32 devices in a mesh: front: 4 (over z), row: 4 (over x, core), col: 2 (over y).
Axes of the slice: x: 2, y: 2, z: 4, core: 2. Of those that a mesh axis runs over, the one named last changes fastest.
Arguments:
- own_rows: float32 [4, 1536, 4096], P('front', 'row', 'col'), may hold values from -1.5 to 1.5
- child_rows: float32 [8192, 4096], P(('front', 'row'), 'col'), may hold values from -3 to 3
- child_dest: int32 [8192, 1], P(('front', 'row')), may hold values from 0 to 3; in each aligned block of 512 rows (0 to 511, 512 to 1023, ...) at most 256 rows name the same one
- child_stair: int32 [8192], P(('front', 'row')), may hold values from 0 to 7
Outputs:
- r_factor: float32 [4, 1024, 4096], P('front', 'row', 'col')
The draws below stay inside these ranges and needn't reach their ends.
Inputs may be any that keep to these rules, and one draw needn't show every extreme that they name: `child_dest`: among the 512 rows of one device at most 256 name one parent, and in every draw some device has exactly 256 rows for some parent.
All inputs are finite; a program needn't handle non-finite values.
Results may differ from the reference program's by a relative error of at most 0.0003.
Values sent between devices are 32-bit elements; how exact they have to be, the bound alone decides.
A program may use at most 128 MiB of HBM per device.

```python
import math
import jax
import jax.numpy as jnp
import numpy as np
from jax import lax

NC = 4096
PANEL_COLUMNS = 512
PANEL_COUNT = 2
SRC_DEV = 512
STAIR_BLK = 128
CAP = 256
OWN_ALL = 1536
CHILD_ROWS = 8192
N_FRONT = 4
N_ROW = 4


def place_ends(drawn, stream_key, least, high):
    longest = drawn.shape.index(max(drawn.shape))
    spots = []
    for shift in (0, 1):
        where = [jax.random.randint(jax.random.fold_in(stream_key, axis), (), 0, length) for axis, length in enumerate(drawn.shape)]
        where[longest] = (where[longest] + shift) % drawn.shape[longest]
        spots.append(tuple(where))
    return drawn.at[spots[0]].set(least).at[spots[1]].set(high)


def block_scale(key, dims, split, low, top_value):
    def one(dim, blocks):
        heights = jax.random.uniform(jax.random.fold_in(jax.random.fold_in(key, 6), dim), (blocks,), jnp.float32, low / len(split), top_value / len(split))
        return jnp.repeat(jnp.exp(heights), dims[dim] // blocks).reshape((-1,) + (1,) * (len(dims) - dim - 1))

    level = one(*split[0])
    for cut in split[1:]:
        level = level * one(*cut)
    return level


def deal_out(stream_key, own, number, rows, count, top, limit, lean):
    ranking = jax.random.permutation(stream_key, count)
    packed, ordinary = portions_of(count, rows * top, limit, lean, True), portions_of(count, rows * top, limit, lean, False)
    places = jnp.arange(count)

    def named(tallies, offset_by):
        used = int((tallies > 0).sum())
        fixed = max(1, used // 4)
        passed = fixed + (places - fixed + offset_by * (used - fixed)) % max(1, count - fixed)
        return jnp.zeros((count,), jnp.int32).at[ranking[jnp.where(places < fixed, places, passed)]].set(jnp.asarray(tallies, jnp.int32))

    tallies = jnp.where(number % 4 == 0, named(packed, number // 4), named(ordinary, number - number // 4 - 1))
    mixed = jax.random.permutation(jax.random.fold_in(own, 3), count)
    giver, receiver = mixed[0:count // 2 * 2:2], mixed[1:count // 2 * 2:2]
    margin = jnp.minimum(tallies[giver] - 1, limit - tallies[receiver]) // 2
    margin = jnp.where((giver == ranking[0]) | (receiver == ranking[0]) | (tallies[receiver] == 0), 0, jnp.maximum(margin, 0))
    passed = jax.random.randint(jax.random.fold_in(own, 4), (count // 2,), 0, 1 << 20) % (margin + 1)
    tallies = tallies.at[giver].add(-passed).at[receiver].add(passed)
    labels = jnp.searchsorted(jnp.cumsum(tallies), jnp.arange(rows * top), side="right").astype(jnp.int32)
    grid = labels.reshape(top, rows).T
    grid = grid[jax.random.permutation(jax.random.fold_in(own, 1), rows)]
    offset_by = jax.random.randint(jax.random.fold_in(own, 2), (rows, 1), 0, top)
    return jnp.take_along_axis(grid, (jnp.arange(top)[None, :] + offset_by) % top, axis=1)


def portions_of(number_of, total, reach, slope, full):
    weights = [(1 << 20) // math.isqrt(grade ** slope) + 1 for grade in range(1, number_of + 1)]
    largest = reach if full else min(reach, max(-(-total // number_of), total * weights[0] // sum(weights)))
    least = 1 if total - largest >= number_of - 1 else 0
    counts, rest = [largest] + [least] * (number_of - 1), total - largest - least * (number_of - 1)
    while rest > 0:
        free = [i for i in range(1, number_of) if counts[i] < largest] or [i for i in range(1, number_of) if counts[i] < reach]
        whole, remaining = sum([weights[i] for i in free]), rest
        for i in free:
            extra = min(reach - counts[i], max(1, remaining * weights[i] // whole), rest)
            counts[i] = counts[i] + extra
            rest = rest - extra
    return np.array(counts)


def bell_draw(own_key, extent, width, most, pieces=(), kind=jnp.bfloat16):
    result = jax.random.normal(own_key, extent, jnp.float32) * width
    if len(pieces) > 0:
        result = block_scale(own_key, extent, pieces, -0.22, 0.18) * result
    return jnp.clip(result, min=-most, max=most).astype(kind)


def setup_inputs(seed: int = 0) -> dict:
    keys = jax.random.split(jax.random.key(seed), 5)
    own_rows = bell_draw(keys[0], (N_FRONT, OWN_ALL, NC), 0.25, 1.5, ((0, 4), (1, 4), (2, 2)), jnp.float32)
    child_rows = bell_draw(keys[1], (CHILD_ROWS, NC), 0.5, 3.0, ((0, 16), (1, 2)), jnp.float32)
    child_dest_keys = jax.random.split(jax.random.fold_in(keys[2], 1), CHILD_ROWS // SRC_DEV)
    child_dest_turns = jax.random.permutation(jax.random.fold_in(keys[2], 3), CHILD_ROWS // SRC_DEV)
    child_dest = jax.vmap(lambda own, number: deal_out(jax.random.fold_in(keys[2], 2), own, number, SRC_DEV, N_FRONT, 1, CAP, 1))(child_dest_keys, child_dest_turns).reshape((CHILD_ROWS, 1))
    child_stair = place_ends(jax.random.randint(keys[3], (CHILD_ROWS,), 0, 8), jax.random.fold_in(keys[3], 1), 0, 7).astype(jnp.int32)
    return {"own_rows": own_rows, "child_rows": child_rows, "child_dest": child_dest, "child_stair": child_stair}


def reference(own_rows, child_rows, child_dest, child_stair):
    columns = jnp.arange(NC, dtype=jnp.int32)
    kept_mask = columns[None, :] >= (child_stair * STAIR_BLK)[:, None]
    masked_rows = jnp.where(kept_mask, child_rows, jnp.zeros_like(child_rows))
    targets = child_dest[:, 0]
    bound_rows = N_FRONT * N_ROW * CAP
    eliminated_panel = PANEL_COUNT * PANEL_COLUMNS

    def one_parent(parent):
        hits = targets == parent
        position = jnp.nonzero(hits, size=bound_rows, fill_value=0)[0].astype(jnp.int32)
        is_valid = jnp.arange(bound_rows, dtype=jnp.int32) < jnp.sum(hits.astype(jnp.int32))
        picked_rows = jnp.where(is_valid[:, None], masked_rows[position], jnp.zeros((bound_rows, NC), masked_rows.dtype))
        stacked_rows = jnp.concatenate([own_rows[parent], picked_rows], 0)
        gramian_block = jnp.dot(stacked_rows[:, :eliminated_panel].T, stacked_rows, precision=lax.Precision.HIGHEST, preferred_element_type=masked_rows.dtype)
        lower_cholesky_factor = jnp.linalg.cholesky(gramian_block[:, :eliminated_panel])
        return jax.scipy.linalg.solve_triangular(lower_cholesky_factor, gramian_block, lower=True)
    return lax.map(one_parent, jnp.arange(N_FRONT, dtype=jnp.int32))
```

```python
import functools

import jax
import jax.numpy as jnp
from jax import lax
from jax.experimental import pallas as pl
from jax.experimental.pallas import tpu as pltpu
from jax.sharding import PartitionSpec as P

PANEL_COLUMNS = 512
PANEL_COUNT = 2
STAIR_BLK = 128
BLOCK = 128
HALF = 64
HI = lax.Precision.HIGHEST
TN = (((0,), (0,)), ((), ()))
NT = (((1,), (1,)), ((), ()))


def mm(a, b, dims=(((1,), (0,)), ((), ()))):
    return lax.dot_general(a, b, dims, precision=HI, preferred_element_type=jnp.float32)


def split(x):
    hi = x.astype(jnp.bfloat16)
    return hi, (x - hi.astype(jnp.float32)).astype(jnp.bfloat16)


def gram_kernel(own_lhs, child_lhs, own_rhs, child_rhs, out, lhs_hi, lhs_lo):
    n_own = own_lhs.shape[1]

    @pl.when(pl.program_id(0) == 0)
    def _():
        for src, start in ((own_lhs, 0), (child_lhs, n_own)):
            rows = src.shape[1]
            hi, lo = split(src[0])
            lhs_hi[start : start + rows] = hi
            lhs_lo[start : start + rows] = lo

    own_hi, own_lo = split(own_rhs[0])
    child_hi, child_lo = split(child_rhs[0])
    rhs_hi = jnp.concatenate([own_hi, child_hi], 0)
    rhs_lo = jnp.concatenate([own_lo, child_lo], 0)

    def dot(a, b):
        return lax.dot_general(a, b, TN, preferred_element_type=jnp.float32)

    width = 256
    for start in range(0, out.shape[1], width):
        cols = slice(start, start + width)
        a_hi, a_lo = lhs_hi[:, cols], lhs_lo[:, cols]
        out[0, cols, :] = dot(a_lo, rhs_hi) + dot(a_hi, rhs_lo) + dot(a_hi, rhs_hi)


def gram(own, child, eliminated, parts):
    n_col, own_rows, half_cols = own.shape
    child_rows = child.shape[1]
    per = parts // n_col
    width = half_cols // per
    return pl.pallas_call(
        gram_kernel,
        out_shape=jax.ShapeDtypeStruct((parts, eliminated, width), jnp.float32),
        grid=(parts,),
        in_specs=[
            pl.BlockSpec((1, own_rows, eliminated), lambda q: (0, 0, 0)),
            pl.BlockSpec((1, child_rows, eliminated), lambda q: (0, 0, 0)),
            pl.BlockSpec((1, own_rows, width), lambda q: (q // per, 0, q % per)),
            pl.BlockSpec((1, child_rows, width), lambda q: (q // per, 0, q % per)),
        ],
        out_specs=pl.BlockSpec((1, eliminated, width), lambda q: (q, 0, 0)),
        scratch_shapes=[pltpu.VMEM((own_rows + child_rows, eliminated), jnp.bfloat16)] * 2,
        cost_estimate=pl.CostEstimate(
            flops=6 * (own_rows + child_rows) * eliminated * half_cols * n_col,
            bytes_accessed=4 * (own_rows + child_rows + eliminated) * half_cols * n_col,
            transcendentals=0,
        ),
    )(own, child, own, child)


def small_inverse(block):
    lanes = lax.broadcasted_iota(jnp.int32, (HALF, 2 * HALF), 1)
    rows = lax.broadcasted_iota(jnp.int32, (HALF, 2 * HALF), 0)
    eye = (lanes[:, :HALF] == rows[:, :HALF]).astype(jnp.float32)
    both = jnp.concatenate([block, eye], 1)

    def step(j, m):
        pivot_row = jnp.sum(jnp.where(rows == j, m, 0.0), axis=0, keepdims=True)
        column = jnp.sum(jnp.where(lanes == j, m, 0.0), axis=1, keepdims=True)
        pivot = jnp.sum(jnp.where(lanes[:1] == j, pivot_row, 0.0), axis=1, keepdims=True)
        scale = lax.rsqrt(pivot)
        scaled = pivot_row * scale
        factor = column * scale
        return jnp.where(rows > j, m - factor * scaled, jnp.where(rows == j, scaled, m))

    return lax.fori_loop(0, HALF, step, both)[:, HALF:]


def inverse_kernel(blocks, out, work):
    n = out.shape[0]
    width = blocks.shape[2]
    count = n // BLOCK
    for part in range(blocks.shape[0]):
        work[:, part * width : (part + 1) * width] = blocks[part]

    def init(k, carry):
        r = pl.multiple_of(k * BLOCK, BLOCK)
        lanes = lax.broadcasted_iota(jnp.int32, (BLOCK, n), 1)
        rows = lax.broadcasted_iota(jnp.int32, (BLOCK, n), 0)
        work[pl.ds(r, BLOCK), n:] = (lanes == rows + r).astype(jnp.float32)
        return carry

    lax.fori_loop(0, count, init, 0)

    def outer(k, carry):
        r = pl.multiple_of(k * BLOCK, BLOCK)
        d = work[pl.ds(r, BLOCK), pl.ds(r, BLOCK)]
        d12 = d[:HALF, HALF:]
        first = small_inverse(d[:HALF, :HALF])
        r12 = mm(first, d12)
        second = small_inverse(d[HALF:, HALF:] - mm(r12, r12, TN))
        corner = -mm(second, mm(r12, first, TN))
        whole = jnp.concatenate(
            [
                jnp.concatenate([first, jnp.zeros((HALF, HALF), jnp.float32)], 1),
                jnp.concatenate([corner, second], 1),
            ],
            0,
        )
        work[pl.ds(r, BLOCK), :] = mm(whole, work[pl.ds(r, BLOCK), :])

        def inner(j, c):
            s = pl.multiple_of(j * BLOCK, BLOCK)
            top = work[pl.ds(r, BLOCK), :]
            left = work[pl.ds(r, BLOCK), pl.ds(s, BLOCK)]
            work[pl.ds(s, BLOCK), :] = work[pl.ds(s, BLOCK), :] - mm(left, top, TN)
            return c

        lax.fori_loop(k + 1, count, inner, 0)
        return carry

    lax.fori_loop(0, count, outer, 0)
    out[...] = work[:, n:]


def cholesky_inverse(blocks):
    n = blocks.shape[1]
    return pl.pallas_call(
        inverse_kernel,
        out_shape=jax.ShapeDtypeStruct((n, n), jnp.float32),
        in_specs=[pl.BlockSpec(memory_space=pltpu.VMEM)],
        out_specs=pl.BlockSpec(memory_space=pltpu.VMEM),
        scratch_shapes=[pltpu.VMEM((n, 2 * n), jnp.float32)],
        cost_estimate=pl.CostEstimate(
            flops=80 * n * n * n, bytes_accessed=8 * n * n, transcendentals=n
        ),
    )(blocks)


def body(own_rows, child_rows, child_dest, child_stair):
    n_front = lax.axis_size("front")
    row_count = lax.axis_size("row")
    n_col = lax.axis_size("col")
    source_rows, half_cols = child_rows.shape
    capacity = max(2, 2 * source_rows // n_front)
    col_index = lax.axis_index("col")
    global_cols = col_index * half_cols + lax.broadcasted_iota(
        jnp.int32, (source_rows, half_cols), 1
    )
    masked_rows = jnp.where(global_cols >= (child_stair * STAIR_BLK)[:, None], child_rows, 0.0)
    targets = child_dest[:, 0]
    onehot = (targets[:, None] == jnp.arange(n_front, dtype=jnp.int32)[None, :]).astype(jnp.int32)
    slot = jnp.sum((jnp.cumsum(onehot, axis=0) - onehot) * onehot, axis=1)
    eliminated = PANEL_COUNT * PANEL_COLUMNS
    parts = row_count * n_col
    sub_cap = capacity // n_col
    position = (slot % n_col) * (n_front * sub_cap) + targets * sub_cap + slot // n_col
    send_block = (
        jnp.zeros((n_front * capacity, half_cols), jnp.float32).at[position].set(masked_rows)
    )
    child = lax.all_to_all(send_block, ("col", "front"), split_axis=0, concat_axis=0, tiled=True)
    child = child.reshape(n_col, n_front * sub_cap, half_cols)
    own = lax.all_to_all(own_rows[0], "col", split_axis=0, concat_axis=0, tiled=True)
    own = own.reshape(n_col, own_rows.shape[1] // n_col, half_cols)
    products = gram(own, child, eliminated, parts)
    square_parts = eliminated * parts // (n_col * half_cols)
    square = lax.psum(products[:square_parts], ("col", "row"))
    products, square = lax.optimization_barrier((products, square))
    mine = lax.psum_scatter(products, ("col", "row"), scatter_dimension=0, tiled=True)[0]
    inverse = cholesky_inverse(square)
    factor = jnp.dot(inverse, mine, precision=HI, preferred_element_type=jnp.float32)
    factor = lax.all_to_all(
        factor, "row", split_axis=0, concat_axis=1, tiled=True
    )
    return factor[None]


def solution(mesh):
    placed = (
        P("front", "row", "col"),
        P(("front", "row"), "col"),
        P(("front", "row"), None),
        P(("front", "row")),
    )
    return jax.shard_map(
        body, mesh=mesh, in_specs=placed, out_specs=P("front", "row", "col"), check_vma=False
    )
```

```python
import jax
import jax.numpy as jnp
from jax import lax
from jax.experimental import pallas as pl
from jax.experimental.pallas import tpu as pltpu
from jax.sharding import PartitionSpec as P

PANEL_COLUMNS = 512
PANEL_COUNT = 2
STAIR_BLK = 128
BLOCK = 128
HALF = 64
TILE = 256
HI = lax.Precision.HIGHEST
TN = (((0,), (0,)), ((), ()))
NN = (((1,), (0,)), ((), ()))


def mm(a, b, dims=NN):
    return lax.dot_general(a, b, dims, precision=HI, preferred_element_type=jnp.float32)


def split(x):
    hi = x.astype(jnp.bfloat16)
    return hi, (x - hi.astype(jnp.float32)).astype(jnp.bfloat16)


def dot3(a, b, dims):
    a_hi, a_lo = a
    b_hi, b_lo = b

    def dot(x, y):
        return lax.dot_general(x, y, dims, preferred_element_type=jnp.float32)

    return dot(a_lo, b_hi) + dot(a_hi, b_lo) + dot(a_hi, b_hi)


def packed_index(row, col):
    return col * (col + 1) // 2 + row


def gram_kernel(own_lhs, child_lhs, own_rhs, child_rhs, out, square, lhs_hi, lhs_lo):
    n_own = own_lhs.shape[1]
    eliminated = out.shape[1]
    width = out.shape[2]

    @pl.when(pl.program_id(0) == 0)
    def _():
        for src, start in ((own_lhs, 0), (child_lhs, n_own)):
            rows = src.shape[1]
            hi, lo = split(src[0])
            lhs_hi[start : start + rows] = hi
            lhs_lo[start : start + rows] = lo

    own_hi, own_lo = split(own_rhs[0])
    child_hi, child_lo = split(child_rhs[0])
    rhs = (jnp.concatenate([own_hi, child_hi], 0), jnp.concatenate([own_lo, child_lo], 0))
    for start in range(0, eliminated, TILE):
        cols = slice(start, start + TILE)
        out[0, cols, :] = dot3((lhs_hi[:, cols], lhs_lo[:, cols]), rhs, TN)

    for part in range(eliminated // width):

        @pl.when(pl.program_id(0) == part)
        def _():
            for local in range(width // TILE):
                col = part * (width // TILE) + local
                for row in range(col + 1):
                    square[packed_index(row, col)] = out[
                        0, row * TILE : (row + 1) * TILE, local * TILE : (local + 1) * TILE
                    ]


def gram(own, child, eliminated, parts):
    n_col, own_rows, half_cols = own.shape
    child_rows = child.shape[1]
    per = parts // n_col
    width = half_cols // per
    tiles = packed_index(0, eliminated // TILE)
    return pl.pallas_call(
        gram_kernel,
        out_shape=(
            jax.ShapeDtypeStruct((parts, eliminated, width), jnp.float32),
            jax.ShapeDtypeStruct((tiles, TILE, TILE), jnp.float32),
        ),
        grid=(parts,),
        in_specs=[
            pl.BlockSpec((1, own_rows, eliminated), lambda q: (0, 0, 0)),
            pl.BlockSpec((1, child_rows, eliminated), lambda q: (0, 0, 0)),
            pl.BlockSpec((1, own_rows, width), lambda q: (q // per, 0, q % per)),
            pl.BlockSpec((1, child_rows, width), lambda q: (q // per, 0, q % per)),
        ],
        out_specs=(
            pl.BlockSpec((1, eliminated, width), lambda q: (q, 0, 0)),
            pl.BlockSpec((tiles, TILE, TILE), lambda q: (0, 0, 0)),
        ),
        scratch_shapes=[pltpu.VMEM((own_rows + child_rows, eliminated), jnp.bfloat16)] * 2,
        cost_estimate=pl.CostEstimate(
            flops=6 * (own_rows + child_rows) * eliminated * half_cols * n_col,
            bytes_accessed=4 * (own_rows + child_rows + eliminated) * half_cols * n_col,
            transcendentals=0,
        ),
    )(own, child, own, child)


def small_inverse(block):
    lanes = lax.broadcasted_iota(jnp.int32, (HALF, HALF), 1)
    rows = lax.broadcasted_iota(jnp.int32, (HALF, HALF), 0)
    eye = (lanes == rows).astype(jnp.float32)
    both = jnp.concatenate([block, eye], 1)
    groups = [both[g * 8 : (g + 1) * 8] for g in range(HALF // 8)]
    sub = lax.broadcasted_iota(jnp.int32, (8, 1), 0)
    for j in range(HALF):
        home, inside = divmod(j, 8)
        pivot_row = groups[home][inside : inside + 1]
        pivot = pivot_row[:, j : j + 1]
        reduced = pivot_row * (1.0 / pivot)
        scaled = pivot_row * lax.rsqrt(pivot)
        for g in range(home, HALF // 8):
            column = groups[g][:, j : j + 1]
            updated = groups[g] - column * reduced
            if g == home:
                kept = jnp.where(sub == inside, scaled, groups[g])
                updated = jnp.where(sub > inside, updated, kept)
            groups[g] = updated
    return jnp.concatenate(groups, 0)[:, HALF:]


def inverse_kernel(blocks, out, work):
    n = out.shape[0]
    count = n // BLOCK
    for col in range(n // TILE):
        for row in range(col + 1):
            work[row * TILE : (row + 1) * TILE, col * TILE : (col + 1) * TILE] = blocks[
                packed_index(row, col)
            ]
    lanes = lax.broadcasted_iota(jnp.int32, (BLOCK, n), 1)
    rows = lax.broadcasted_iota(jnp.int32, (BLOCK, n), 0)

    def outer(k, carry):
        r = pl.multiple_of(k * BLOCK, BLOCK)
        d = work[pl.ds(r, BLOCK), pl.ds(r, BLOCK)]
        first = small_inverse(d[:HALF, :HALF])
        r12 = mm(first, d[:HALF, HALF:])
        second = small_inverse(d[HALF:, HALF:] - mm(r12, r12, TN))
        corner = -mm(second, mm(r12, first, TN))
        whole = jnp.concatenate(
            [
                jnp.concatenate([first, jnp.zeros((HALF, HALF), jnp.float32)], 1),
                jnp.concatenate([corner, second], 1),
            ],
            0,
        )
        here = (lanes >= r) & (lanes < r + BLOCK)
        top = jnp.where(here, (lanes == rows + r).astype(jnp.float32), work[pl.ds(r, BLOCK), :])
        top = dot3(split(whole), split(top), NN)
        work[pl.ds(r, BLOCK), :] = top

        def inner(j, c):
            s = pl.multiple_of(j * BLOCK, BLOCK)
            left = split(work[pl.ds(r, BLOCK), pl.ds(s, BLOCK)])
            right = split(work[pl.ds(r, BLOCK), :])
            kept = jnp.where(here, 0.0, work[pl.ds(s, BLOCK), :])
            work[pl.ds(s, BLOCK), :] = kept - dot3(left, right, TN)
            return c

        lax.fori_loop(k + 1, count, inner, 0)
        return carry

    lax.fori_loop(0, count, outer, 0)

    def finish(k, carry):
        r = pl.multiple_of(k * BLOCK, BLOCK)
        out[pl.ds(r, BLOCK), :] = jnp.where(lanes <= rows + r, work[pl.ds(r, BLOCK), :], 0.0)
        return carry

    lax.fori_loop(0, count, finish, 0)


def cholesky_inverse(blocks, n):
    return pl.pallas_call(
        inverse_kernel,
        out_shape=jax.ShapeDtypeStruct((n, n), jnp.float32),
        in_specs=[pl.BlockSpec(memory_space=pltpu.VMEM)],
        out_specs=pl.BlockSpec(memory_space=pltpu.VMEM),
        scratch_shapes=[pltpu.VMEM((n, n), jnp.float32)],
        cost_estimate=pl.CostEstimate(
            flops=80 * n * n * n, bytes_accessed=8 * n * n, transcendentals=n
        ),
    )(blocks)


def exchange_own(rows, n_col, col_index):
    share = rows.shape[0] // n_col
    arrived = [lax.dynamic_slice_in_dim(rows, col_index * share, share, 0)]
    for shift in range(1, n_col):
        leaving = lax.dynamic_slice_in_dim(rows, (col_index + shift) % n_col * share, share, 0)
        arrived.append(
            lax.ppermute(leaving, "col", [(i, (i + shift) % n_col) for i in range(n_col)])
        )
    blocks = []
    for source in range(n_col):
        block = arrived[0]
        for shift in range(1, n_col):
            block = jnp.where((source + shift) % n_col == col_index, arrived[shift], block)
        blocks.append(block)
    return jnp.stack(blocks)


def body(own_rows, child_rows, child_dest, child_stair):
    n_front = lax.axis_size("front")
    row_count = lax.axis_size("row")
    n_col = lax.axis_size("col")
    source_rows, half_cols = child_rows.shape
    capacity = max(2, 2 * source_rows // n_front)
    col_index = lax.axis_index("col")
    own = exchange_own(own_rows[0], n_col, col_index)
    global_cols = col_index * half_cols + lax.broadcasted_iota(
        jnp.int32, (source_rows, half_cols), 1
    )
    masked_rows = jnp.where(global_cols >= (child_stair * STAIR_BLK)[:, None], child_rows, 0.0)
    targets = child_dest[:, 0]
    onehot = (targets[:, None] == jnp.arange(n_front, dtype=jnp.int32)[None, :]).astype(jnp.int32)
    slot = jnp.sum((jnp.cumsum(onehot, axis=0) - onehot) * onehot, axis=1)
    eliminated = PANEL_COUNT * PANEL_COLUMNS
    parts = row_count * n_col
    sub_cap = capacity // n_col
    position = (slot % n_col) * (n_front * sub_cap) + targets * sub_cap + slot // n_col
    send_block = (
        jnp.zeros((n_front * capacity, half_cols), jnp.float32).at[position].set(masked_rows)
    )
    child = lax.all_to_all(send_block, ("col", "front"), split_axis=0, concat_axis=0, tiled=True)
    child = child.reshape(n_col, n_front * sub_cap, half_cols)
    products, square = gram(own, child, eliminated, parts)
    square = lax.psum(square, ("col", "row"))
    products, square = lax.optimization_barrier((products, square))
    mine = lax.psum_scatter(products, ("col", "row"), scatter_dimension=0, tiled=True)[0]
    inverse = cholesky_inverse(square, eliminated)
    factor = jnp.dot(
        inverse, mine, precision=lax.Precision.HIGH, preferred_element_type=jnp.float32
    )
    factor = lax.all_to_all(
        factor, "row", split_axis=0, concat_axis=1, tiled=True
    )
    return factor[None]


def solution(mesh):
    placed = (
        P("front", "row", "col"),
        P(("front", "row"), "col"),
        P(("front", "row"), None),
        P(("front", "row")),
    )
    return jax.shard_map(
        body, mesh=mesh, in_specs=placed, out_specs=P("front", "row", "col"), check_vma=False
    )
```

```python
import jax
import jax.numpy as jnp
from jax import lax
from jax.experimental import pallas as pl
from jax.experimental.pallas import tpu as pltpu
from jax.sharding import PartitionSpec as P

PANEL_COLUMNS = 512
PANEL_COUNT = 2
STAIR_BLK = 128
BLOCK = 128
HALF = 64
TILE = 256
HI = lax.Precision.HIGHEST
TN = (((0,), (0,)), ((), ()))
NN = (((1,), (0,)), ((), ()))


def mm(a, b, dims=NN):
    return lax.dot_general(a, b, dims, precision=HI, preferred_element_type=jnp.float32)


def split(x):
    hi = x.astype(jnp.bfloat16)
    return hi, (x - hi.astype(jnp.float32)).astype(jnp.bfloat16)


def dot3(a, b, dims):
    a_hi, a_lo = a
    b_hi, b_lo = b

    def dot(x, y):
        return lax.dot_general(x, y, dims, preferred_element_type=jnp.float32)

    return dot(a_lo, b_hi) + dot(a_hi, b_lo) + dot(a_hi, b_hi)


def packed_index(row, col):
    return col * (col + 1) // 2 + row


def gram_kernel(own_lhs, child_lhs, *refs):
    *rhs_refs, out, square, lhs_hi, lhs_lo = refs
    n_own = own_lhs.shape[1]
    eliminated = out.shape[1]
    tiles = eliminated // TILE

    @pl.when(pl.program_id(0) == 0)
    def _():
        for src, start in ((own_lhs, 0), (child_lhs, n_own)):
            rows = src.shape[1]
            hi, lo = split(src[0])
            lhs_hi[start : start + rows] = hi
            lhs_lo[start : start + rows] = lo

    half = len(rhs_refs) // 2
    own_rhs = jnp.concatenate([ref[0] for ref in rhs_refs[:half]], 1)
    child_rhs = jnp.concatenate([ref[0] for ref in rhs_refs[half:]], 1)
    rhs = split(jnp.concatenate([own_rhs, child_rhs], 0))

    def lhs(row):
        cols = slice(row * TILE, (row + 1) * TILE)
        return lhs_hi[:, cols], lhs_lo[:, cols]

    for row in range(tiles):
        out[0, row * TILE : (row + 1) * TILE, :] = dot3(lhs(row), rhs, TN)

    for col in range(tiles):

        @pl.when(pl.program_id(0) == col)
        def _():
            for row in range(col + 1):
                square[packed_index(row, col)] = dot3(lhs(row), lhs(col), TN)


def gram(own, child, eliminated, parts):
    n_col, own_rows, half_cols = own.shape
    child_rows = child.shape[1]
    widths = [(half_cols - (eliminated if c == 0 else 0)) // parts for c in range(n_col)]
    skips = [eliminated // widths[0]] + [0] * (n_col - 1)
    tiles = packed_index(0, eliminated // TILE)

    def pieces(rows):
        return [
            pl.BlockSpec((1, rows, widths[c]), lambda q, c=c: (c, 0, skips[c] + q))
            for c in range(n_col)
        ]

    return pl.pallas_call(
        gram_kernel,
        out_shape=(
            jax.ShapeDtypeStruct((parts, eliminated, sum(widths)), jnp.float32),
            jax.ShapeDtypeStruct((tiles, TILE, TILE), jnp.float32),
        ),
        grid=(parts,),
        in_specs=[
            pl.BlockSpec((1, own_rows, eliminated), lambda q: (0, 0, 0)),
            pl.BlockSpec((1, child_rows, eliminated), lambda q: (0, 0, 0)),
        ]
        + pieces(own_rows)
        + pieces(child_rows),
        out_specs=(
            pl.BlockSpec((1, eliminated, sum(widths)), lambda q: (q, 0, 0)),
            pl.BlockSpec((tiles, TILE, TILE), lambda q: (0, 0, 0)),
        ),
        scratch_shapes=[pltpu.VMEM((own_rows + child_rows, eliminated), jnp.bfloat16)] * 2,
        cost_estimate=pl.CostEstimate(
            flops=6 * (own_rows + child_rows) * eliminated * half_cols * n_col,
            bytes_accessed=4 * (own_rows + child_rows + eliminated) * half_cols * n_col,
            transcendentals=0,
        ),
    )(own, child, *([own] * n_col), *([child] * n_col))


def small_inverse(block):
    lanes = lax.broadcasted_iota(jnp.int32, (HALF, HALF), 1)
    rows = lax.broadcasted_iota(jnp.int32, (HALF, HALF), 0)
    eye = (lanes == rows).astype(jnp.float32)
    both = jnp.concatenate([block, eye], 1)
    count = HALF // 8
    groups = [both[g * 8 : (g + 1) * 8] for g in range(count)]
    sub = lax.broadcasted_iota(jnp.int32, (8, 2 * HALF), 0)

    def column_of(g, j):
        return jnp.broadcast_to(groups[g][:, j : j + 1], (8, 2 * HALF))

    def row_of(x, s):
        return jnp.broadcast_to(x[s : s + 1], x.shape)

    for home in range(count):
        first = home * 8
        below = [[column_of(g, first + s) for s in range(8)] for g in range(home + 1, count)]
        columns = [column_of(home, first + s) for s in range(8)]
        solved = forward = groups[home]
        pivots = columns[0]
        for s in range(8):
            column = columns[s]
            pivot = row_of(column, s)
            inverse = 1.0 / pivot
            pivots = jnp.where(sub == s, pivot, pivots)
            forward = jnp.where(
                sub > s, forward - column * (row_of(forward, s) * inverse), forward
            )
            scaled = row_of(solved, s) * inverse
            solved = jnp.where(sub == s, scaled, solved - column * scaled)
            for t in range(s + 1, 8):
                scaled = row_of(columns[t], s) * inverse
                columns[t] = jnp.where(sub == s, scaled, columns[t] - column * scaled)
        groups[home] = forward * lax.rsqrt(pivots)
        spread = [row_of(solved, s) for s in range(8)]
        for g in range(home + 1, count):
            terms = [below[g - home - 1][s] * spread[s] for s in range(8)]
            while len(terms) > 1:
                terms = [terms[i] + terms[i + 1] for i in range(0, len(terms), 2)]
            groups[g] = groups[g] - terms[0]
    return jnp.concatenate(groups, 0)[:, HALF:]


def inverse_kernel(blocks, out, upper, work):
    n = out.shape[0]
    count = n // BLOCK
    for col in range(n // TILE):
        for row in range(col + 1):
            work[row * TILE : (row + 1) * TILE, col * TILE : (col + 1) * TILE] = blocks[
                packed_index(row, col)
            ]
    lanes = lax.broadcasted_iota(jnp.int32, (BLOCK, n), 1)
    rows = lax.broadcasted_iota(jnp.int32, (BLOCK, n), 0)

    def outer(k, carry):
        r = pl.multiple_of(k * BLOCK, BLOCK)
        d = work[pl.ds(r, BLOCK), pl.ds(r, BLOCK)]
        first = small_inverse(d[:HALF, :HALF])
        r12 = mm(first, d[:HALF, HALF:])
        second = small_inverse(d[HALF:, HALF:] - mm(r12, r12, TN))
        corner = -mm(second, mm(r12, first, TN))
        whole = jnp.concatenate(
            [
                jnp.concatenate([first, jnp.zeros((HALF, HALF), jnp.float32)], 1),
                jnp.concatenate([corner, second], 1),
            ],
            0,
        )
        here = (lanes >= r) & (lanes < r + BLOCK)
        top = dot3(split(whole), split(work[pl.ds(r, BLOCK), :]), NN)
        upper[pl.ds(r, BLOCK), :] = jnp.where(lanes >= rows + r, top, 0.0)
        work[pl.ds(r, BLOCK), :] = top
        work[pl.ds(r, BLOCK), pl.ds(r, BLOCK)] = whole

        def inner(j, c):
            s = pl.multiple_of(j * BLOCK, BLOCK)
            left = split(work[pl.ds(r, BLOCK), pl.ds(s, BLOCK)])
            right = split(work[pl.ds(r, BLOCK), :])
            kept = jnp.where(here, 0.0, work[pl.ds(s, BLOCK), :])
            work[pl.ds(s, BLOCK), :] = kept - dot3(left, right, TN)
            return c

        lax.fori_loop(k + 1, count, inner, 0)
        return carry

    lax.fori_loop(0, count, outer, 0)

    def finish(k, carry):
        r = pl.multiple_of(k * BLOCK, BLOCK)
        out[pl.ds(r, BLOCK), :] = jnp.where(lanes <= rows + r, work[pl.ds(r, BLOCK), :], 0.0)
        return carry

    lax.fori_loop(0, count, finish, 0)


def cholesky_inverse(blocks, n):
    return pl.pallas_call(
        inverse_kernel,
        out_shape=(jax.ShapeDtypeStruct((n, n), jnp.float32),) * 2,
        in_specs=[pl.BlockSpec(memory_space=pltpu.VMEM)],
        out_specs=(pl.BlockSpec(memory_space=pltpu.VMEM),) * 2,
        scratch_shapes=[pltpu.VMEM((n, n), jnp.float32)],
        cost_estimate=pl.CostEstimate(
            flops=80 * n * n * n, bytes_accessed=8 * n * n, transcendentals=n
        ),
    )(blocks)


def exchange_own(rows, n_col, col_index):
    share = rows.shape[0] // n_col
    arrived = [lax.dynamic_slice_in_dim(rows, col_index * share, share, 0)]
    for shift in range(1, n_col):
        leaving = lax.dynamic_slice_in_dim(rows, (col_index + shift) % n_col * share, share, 0)
        arrived.append(
            lax.ppermute(leaving, "col", [(i, (i + shift) % n_col) for i in range(n_col)])
        )
    blocks = []
    for source in range(n_col):
        block = arrived[0]
        for shift in range(1, n_col):
            block = jnp.where((source + shift) % n_col == col_index, arrived[shift], block)
        blocks.append(block)
    return jnp.stack(blocks)


def body(own_rows, child_rows, child_dest, child_stair):
    n_front = lax.axis_size("front")
    row_count = lax.axis_size("row")
    n_col = lax.axis_size("col")
    source_rows, half_cols = child_rows.shape
    capacity = max(2, 2 * source_rows // n_front)
    col_index = lax.axis_index("col")
    own = exchange_own(own_rows[0], n_col, col_index)
    global_cols = col_index * half_cols + lax.broadcasted_iota(
        jnp.int32, (source_rows, half_cols), 1
    )
    masked_rows = jnp.where(global_cols >= (child_stair * STAIR_BLK)[:, None], child_rows, 0.0)
    targets = child_dest[:, 0]
    onehot = (targets[:, None] == jnp.arange(n_front, dtype=jnp.int32)[None, :]).astype(jnp.int32)
    slot = jnp.sum((jnp.cumsum(onehot, axis=0) - onehot) * onehot, axis=1)
    eliminated = PANEL_COUNT * PANEL_COLUMNS
    parts = row_count * n_col
    sub_cap = capacity // n_col
    position = (slot % n_col) * (n_front * sub_cap) + targets * sub_cap + slot // n_col
    send_block = (
        jnp.zeros((n_front * capacity, half_cols), jnp.float32).at[position].set(masked_rows)
    )
    child = lax.all_to_all(send_block, ("col", "front"), split_axis=0, concat_axis=0, tiled=True)
    child = child.reshape(n_col, n_front * sub_cap, half_cols)
    products, square = gram(own, child, eliminated, parts)
    square = lax.psum(square, ("col", "row"))
    products, square = lax.optimization_barrier((products, square))
    mine = lax.psum_scatter(products, ("col", "row"), scatter_dimension=0, tiled=True)[0]
    inverse, upper = cholesky_inverse(square, eliminated)
    factor = jnp.dot(
        inverse, mine, precision=lax.Precision.HIGH, preferred_element_type=jnp.float32
    )
    share = eliminated // parts
    part = col_index * row_count + lax.axis_index("row")
    piece = lax.dynamic_slice_in_dim(upper, part * share, share, 1)
    width = half_cols // parts
    factor = jnp.concatenate([piece, factor], 1)
    blocks = [factor[:, c * width : (c + 1) * width] for c in range(n_col)]
    factor = jnp.stack(blocks).reshape(parts, eliminated // row_count, width)
    factor = lax.all_to_all(factor, ("col", "row"), split_axis=0, concat_axis=0, tiled=True)
    plain = factor.transpose(1, 0, 2).reshape(-1, half_cols)
    mixed = jnp.concatenate(
        [
            factor[:, :, :share].transpose(1, 0, 2).reshape(-1, eliminated),
            factor[:, :, share:].transpose(1, 0, 2).reshape(-1, half_cols - eliminated),
        ],
        1,
    )
    return jnp.where(col_index == 0, mixed, plain)[None]


def solution(mesh):
    placed = (
        P("front", "row", "col"),
        P(("front", "row"), "col"),
        P(("front", "row"), None),
        P(("front", "row")),
    )
    return jax.shard_map(
        body, mesh=mesh, in_specs=placed, out_specs=P("front", "row", "col"), check_vma=False
    )
```

```python
import jax
import jax.numpy as jnp
from jax import lax
from jax.experimental import pallas as pl
from jax.experimental.pallas import tpu as pltpu
from jax.sharding import PartitionSpec as P

PANEL_COLUMNS = 512
PANEL_COUNT = 2
STAIR_BLK = 128
BLOCK = 128
HALF = 64
TILE = 256
HI = lax.Precision.HIGHEST
TN = (((0,), (0,)), ((), ()))
NN = (((1,), (0,)), ((), ()))


def mm(a, b, dims=NN):
    return lax.dot_general(a, b, dims, precision=HI, preferred_element_type=jnp.float32)


def split(x):
    hi = x.astype(jnp.bfloat16)
    return hi, (x - hi.astype(jnp.float32)).astype(jnp.bfloat16)


def dot3(a, b, dims):
    a_hi, a_lo = a
    b_hi, b_lo = b

    def dot(x, y):
        return lax.dot_general(x, y, dims, preferred_element_type=jnp.float32)

    return dot(a_lo, b_hi) + dot(a_hi, b_lo) + dot(a_hi, b_hi)


def packed_index(row, col):
    return col * (col + 1) // 2 + row


def gram_kernel(own_lhs, child_lhs, *refs):
    *rhs_refs, out, square, lhs_hi, lhs_lo = refs
    n_own = own_lhs.shape[1]
    eliminated = out.shape[1]
    tiles = eliminated // TILE

    @pl.when(pl.program_id(0) == 0)
    def _():
        for src, start in ((own_lhs, 0), (child_lhs, n_own)):
            rows = src.shape[1]
            hi, lo = split(src[0])
            lhs_hi[start : start + rows] = hi
            lhs_lo[start : start + rows] = lo

    half = len(rhs_refs) // 2
    own_rhs = jnp.concatenate([ref[0] for ref in rhs_refs[:half]], 1)
    child_rhs = jnp.concatenate([ref[0] for ref in rhs_refs[half:]], 1)
    rhs = split(jnp.concatenate([own_rhs, child_rhs], 0))

    def lhs(row):
        cols = slice(row * TILE, (row + 1) * TILE)
        return lhs_hi[:, cols], lhs_lo[:, cols]

    for row in range(tiles):
        out[0, row * TILE : (row + 1) * TILE, :] = dot3(lhs(row), rhs, TN)

    for col in range(tiles):

        @pl.when(pl.program_id(0) == col)
        def _():
            for row in range(col + 1):
                square[packed_index(row, col)] = dot3(lhs(row), lhs(col), TN)


def gram(own, child, eliminated, parts):
    n_col, own_rows, half_cols = own.shape
    child_rows = child.shape[1]
    widths = [(half_cols - (eliminated if c == 0 else 0)) // parts for c in range(n_col)]
    skips = [eliminated // widths[0]] + [0] * (n_col - 1)
    tiles = packed_index(0, eliminated // TILE)

    def pieces(rows):
        return [
            pl.BlockSpec((1, rows, widths[c]), lambda q, c=c: (c, 0, skips[c] + q))
            for c in range(n_col)
        ]

    return pl.pallas_call(
        gram_kernel,
        out_shape=(
            jax.ShapeDtypeStruct((parts, eliminated, sum(widths)), jnp.float32),
            jax.ShapeDtypeStruct((tiles, TILE, TILE), jnp.float32),
        ),
        grid=(parts,),
        in_specs=[
            pl.BlockSpec((1, own_rows, eliminated), lambda q: (0, 0, 0)),
            pl.BlockSpec((1, child_rows, eliminated), lambda q: (0, 0, 0)),
        ]
        + pieces(own_rows)
        + pieces(child_rows),
        out_specs=(
            pl.BlockSpec((1, eliminated, sum(widths)), lambda q: (q, 0, 0)),
            pl.BlockSpec((tiles, TILE, TILE), lambda q: (0, 0, 0)),
        ),
        scratch_shapes=[pltpu.VMEM((own_rows + child_rows, eliminated), jnp.bfloat16)] * 2,
        cost_estimate=pl.CostEstimate(
            flops=6 * (own_rows + child_rows) * eliminated * half_cols * n_col,
            bytes_accessed=4 * (own_rows + child_rows + eliminated) * half_cols * n_col,
            transcendentals=0,
        ),
    )(own, child, *([own] * n_col), *([child] * n_col))


def small_inverse(block):
    lanes = lax.broadcasted_iota(jnp.int32, (HALF, HALF), 1)
    rows = lax.broadcasted_iota(jnp.int32, (HALF, HALF), 0)
    eye = (lanes == rows).astype(jnp.float32)
    both = jnp.concatenate([block, eye], 1)
    count = HALF // 8
    groups = [both[g * 8 : (g + 1) * 8] for g in range(count)]
    sub = lax.broadcasted_iota(jnp.int32, (8, 2 * HALF), 0)

    def column_of(g, j):
        return jnp.broadcast_to(groups[g][:, j : j + 1], (8, 2 * HALF))

    def row_of(x, s):
        return jnp.broadcast_to(x[s : s + 1], x.shape)

    for home in range(count):
        first = home * 8
        below = [[column_of(g, first + s) for s in range(8)] for g in range(home + 1, count)]
        columns = [column_of(home, first + s) for s in range(8)]
        solved = forward = groups[home]
        pivots = columns[0]
        for s in range(8):
            column = columns[s]
            pivot = row_of(column, s)
            inverse = 1.0 / pivot
            pivots = jnp.where(sub == s, pivot, pivots)
            forward = jnp.where(
                sub > s, forward - column * (row_of(forward, s) * inverse), forward
            )
            scaled = row_of(solved, s) * inverse
            solved = jnp.where(sub == s, scaled, solved - column * scaled)
            for t in range(s + 1, 8):
                scaled = row_of(columns[t], s) * inverse
                columns[t] = jnp.where(sub == s, scaled, columns[t] - column * scaled)
        groups[home] = forward * lax.rsqrt(pivots)
        spread = [row_of(solved, s) for s in range(8)]
        for g in range(home + 1, count):
            terms = [below[g - home - 1][s] * spread[s] for s in range(8)]
            while len(terms) > 1:
                terms = [terms[i] + terms[i + 1] for i in range(0, len(terms), 2)]
            groups[g] = groups[g] - terms[0]
    return jnp.concatenate(groups, 0)[:, HALF:]


def inverse_kernel(blocks, out, upper, work):
    n = out.shape[0]
    count = n // BLOCK
    for col in range(n // TILE):
        for row in range(col + 1):
            work[row * TILE : (row + 1) * TILE, col * TILE : (col + 1) * TILE] = blocks[
                packed_index(row, col)
            ]
    lanes = lax.broadcasted_iota(jnp.int32, (BLOCK, n), 1)
    rows = lax.broadcasted_iota(jnp.int32, (BLOCK, n), 0)

    def outer(k, carry):
        r = pl.multiple_of(k * BLOCK, BLOCK)
        d = work[pl.ds(r, BLOCK), pl.ds(r, BLOCK)]
        first = small_inverse(d[:HALF, :HALF])
        r12 = mm(first, d[:HALF, HALF:])
        second = small_inverse(d[HALF:, HALF:] - mm(r12, r12, TN))
        corner = -mm(second, mm(r12, first, TN))
        whole = jnp.concatenate(
            [
                jnp.concatenate([first, jnp.zeros((HALF, HALF), jnp.float32)], 1),
                jnp.concatenate([corner, second], 1),
            ],
            0,
        )
        here = (lanes >= r) & (lanes < r + BLOCK)
        top = dot3(split(whole), split(work[pl.ds(r, BLOCK), :]), NN)
        upper[pl.ds(r, BLOCK), :] = jnp.where(lanes >= rows + r, top, 0.0)
        work[pl.ds(r, BLOCK), :] = top
        work[pl.ds(r, BLOCK), pl.ds(r, BLOCK)] = whole

        def inner(j, c):
            s = pl.multiple_of(j * BLOCK, BLOCK)
            left = split(work[pl.ds(r, BLOCK), pl.ds(s, BLOCK)])
            right = split(work[pl.ds(r, BLOCK), :])
            kept = jnp.where(here, 0.0, work[pl.ds(s, BLOCK), :])
            work[pl.ds(s, BLOCK), :] = kept - dot3(left, right, TN)
            return c

        lax.fori_loop(k + 1, count, inner, 0)
        return carry

    lax.fori_loop(0, count, outer, 0)

    def finish(k, carry):
        r = pl.multiple_of(k * BLOCK, BLOCK)
        out[pl.ds(r, BLOCK), :] = jnp.where(lanes <= rows + r, work[pl.ds(r, BLOCK), :], 0.0)
        return carry

    lax.fori_loop(0, count, finish, 0)


def cholesky_inverse(blocks, n):
    return pl.pallas_call(
        inverse_kernel,
        out_shape=(jax.ShapeDtypeStruct((n, n), jnp.float32),) * 2,
        in_specs=[pl.BlockSpec(memory_space=pltpu.VMEM)],
        out_specs=(pl.BlockSpec(memory_space=pltpu.VMEM),) * 2,
        scratch_shapes=[pltpu.VMEM((n, n), jnp.float32)],
        cost_estimate=pl.CostEstimate(
            flops=80 * n * n * n, bytes_accessed=8 * n * n, transcendentals=n
        ),
    )(blocks)


def exchange_own(rows, n_col, col_index):
    share = rows.shape[0] // n_col
    arrived = [lax.dynamic_slice_in_dim(rows, col_index * share, share, 0)]
    for shift in range(1, n_col):
        leaving = lax.dynamic_slice_in_dim(rows, (col_index + shift) % n_col * share, share, 0)
        arrived.append(
            lax.ppermute(leaving, "col", [(i, (i + shift) % n_col) for i in range(n_col)])
        )
    blocks = []
    for source in range(n_col):
        block = arrived[0]
        for shift in range(1, n_col):
            block = jnp.where((source + shift) % n_col == col_index, arrived[shift], block)
        blocks.append(block)
    return jnp.stack(blocks)


def assemble_kernel(col_ref, piece, out):
    out[...] = piece[0]


def assemble(factor, col_index, share):
    parts, rows, width = factor.shape
    halves = width // share

    def source(b, col_ref):
        first = col_ref[0] == 0
        part = jnp.where(first, b % parts, b // halves)
        return part, 0, jnp.where(first, b // parts, b % halves)

    return pl.pallas_call(
        assemble_kernel,
        out_shape=jax.ShapeDtypeStruct((rows, parts * width), jnp.float32),
        grid_spec=pltpu.PrefetchScalarGridSpec(
            num_scalar_prefetch=1,
            grid=(parts * halves,),
            in_specs=[pl.BlockSpec((1, rows, share), source)],
            out_specs=pl.BlockSpec((rows, share), lambda b, col_ref: (0, b)),
        ),
    )(col_index.reshape(1).astype(jnp.int32), factor)


def body(own_rows, child_rows, child_dest, child_stair):
    n_front = lax.axis_size("front")
    row_count = lax.axis_size("row")
    n_col = lax.axis_size("col")
    source_rows, half_cols = child_rows.shape
    capacity = max(2, 2 * source_rows // n_front)
    col_index = lax.axis_index("col")
    own = exchange_own(own_rows[0], n_col, col_index)
    global_cols = col_index * half_cols + lax.broadcasted_iota(
        jnp.int32, (source_rows, half_cols), 1
    )
    masked_rows = jnp.where(global_cols >= (child_stair * STAIR_BLK)[:, None], child_rows, 0.0)
    targets = child_dest[:, 0]
    onehot = (targets[:, None] == jnp.arange(n_front, dtype=jnp.int32)[None, :]).astype(jnp.int32)
    slot = jnp.sum((jnp.cumsum(onehot, axis=0) - onehot) * onehot, axis=1)
    eliminated = PANEL_COUNT * PANEL_COLUMNS
    parts = row_count * n_col
    sub_cap = capacity // n_col
    position = (slot % n_col) * (n_front * sub_cap) + targets * sub_cap + slot // n_col
    send_block = (
        jnp.zeros((n_front * capacity, half_cols), jnp.float32).at[position].set(masked_rows)
    )
    child = lax.all_to_all(send_block, ("col", "front"), split_axis=0, concat_axis=0, tiled=True)
    child = child.reshape(n_col, n_front * sub_cap, half_cols)
    products, square = gram(own, child, eliminated, parts)
    square = lax.psum(square, ("col", "row"))
    products, square = lax.optimization_barrier((products, square))
    mine = lax.psum_scatter(products, ("col", "row"), scatter_dimension=0, tiled=True)[0]
    inverse, upper = cholesky_inverse(square, eliminated)
    factor = jnp.dot(
        inverse, mine, precision=lax.Precision.HIGH, preferred_element_type=jnp.float32
    )
    share = eliminated // parts
    part = col_index * row_count + lax.axis_index("row")
    piece = lax.dynamic_slice_in_dim(upper, part * share, share, 1)
    width = half_cols // parts
    factor = jnp.concatenate([piece, factor], 1)
    blocks = [factor[:, c * width : (c + 1) * width] for c in range(n_col)]
    factor = jnp.stack(blocks).reshape(parts, eliminated // row_count, width)
    factor = lax.all_to_all(factor, ("col", "row"), split_axis=0, concat_axis=0, tiled=True)
    return assemble(factor, col_index, share)[None]


def solution(mesh):
    placed = (
        P("front", "row", "col"),
        P(("front", "row"), "col"),
        P(("front", "row"), None),
        P(("front", "row")),
    )
    return jax.shard_map(
        body, mesh=mesh, in_specs=placed, out_specs=P("front", "row", "col"), check_vma=False
    )
```
